256 devices in a mesh: seq: 32 (over x, y, core), ch: 8 (over z).
Axes of the slice: x: 4, y: 4, z: 8, core: 2. Of those that a mesh axis runs over, the one named last changes fastest.
Arguments:
- token_ids: int32 [32768], P('seq'), may hold values from 0 to 511
- embedding: bfloat16 [4096, 512], P('ch'), may hold values from -26 to 26
- projected: bfloat16 [3, 4096, 512], P(None, 'ch'), may hold values from -6 to 6
- short_taps: float32 [7, 3, 4096], P(None, None, 'ch'), may hold values from -2 to 2
- long_filter: bfloat16 [4096, 32768], P('ch', 'seq'), may hold values from -1.6 to 1.6
- skip_gain: float32 [4096], P('ch'), may hold values from -3 to 3
Outputs:
- mixed: bfloat16 [4096, 32768], P('ch', 'seq')
The draws below stay inside these ranges and needn't reach their ends.
All inputs are finite; a program needn't handle non-finite values.
Results may differ from the reference program's by a relative error of at most 0.0075.
Values may be sent and summed in bfloat16 or wider, within the bound.
No kernel may reach another device: no remote copies, remote signals or barrier semaphores. Data moves between devices by JAX's collectives and lax.ppermute only.
A program may use at most 128 MiB of HBM per device.

```python
import math
import jax
import jax.numpy as jnp
import numpy as np
from jax import lax

MIXER_CHANNELS = 4096
VOCAB = 512
TAPS = 7
TOKENS = 32768


def draw_embedding(key, part):
    stochastic_seeds = jax.random.split(key, 3)
    channel_pos = jnp.arange(MIXER_CHANNELS, dtype=jnp.float32)
    rising = 1.0 + 2.0 * channel_pos / (MIXER_CHANNELS - 1)
    channel_scale = jnp.exp(jax.random.uniform(stochastic_seeds[0], (MIXER_CHANNELS, 1), minval=0.0, maxval=math.log(10.0)))
    vocab_factor = jnp.exp(jax.random.uniform(stochastic_seeds[1], (1, VOCAB), minval=math.log(0.7), maxval=math.log(1.4)))
    rough_part = jnp.clip(jax.random.normal(stochastic_seeds[2], (MIXER_CHANNELS, VOCAB)), -6.0, 6.0)
    return (rough_part * channel_scale * rising[:, None] * vocab_factor * 0.1).astype(jnp.bfloat16)


def draw_long_filter(key, part):
    stochastic_seeds = jax.random.split(key, 4)
    filter_extent = TOKENS
    log_rate = jax.random.uniform(stochastic_seeds[0], (MIXER_CHANNELS, 1), minval=math.log(0.1 / filter_extent), maxval=math.log(1.0 / 30.0))
    rough_part = jnp.clip(jax.random.normal(stochastic_seeds[3], (MIXER_CHANNELS, filter_extent)), -6.0, 6.0)
    fading_speed = jnp.exp(log_rate)
    spike_offsets = jnp.arange(filter_extent, dtype=jnp.float32)[None, :]
    fading_profile = -fading_speed * spike_offsets
    spike_onsets = jax.random.randint(stochastic_seeds[1], (MIXER_CHANNELS, 3), 1, filter_extent)
    spike_attenuations = jnp.log(jax.random.uniform(stochastic_seeds[2], (MIXER_CHANNELS, 3), minval=0.5, maxval=0.8))
    for spike_counter in range(3):
        fading_profile = fading_profile + jnp.where(spike_offsets >= spike_onsets[:, spike_counter:spike_counter + 1].astype(jnp.float32), spike_attenuations[:, spike_counter:spike_counter + 1], 0.0)
    normalizer = jnp.sqrt((1.0 - jnp.exp(-2.0 * fading_speed)) / (1.0 - jnp.exp(-2.0 * fading_speed * filter_extent)))
    return (normalizer * jnp.exp(fading_profile) * rough_part).astype(jnp.bfloat16)


def touch_ends(drawn, rng, smallest, top_value):
    dims = drawn.shape
    spot = [jax.random.randint(jax.random.fold_in(rng, axis), (), 0, dims[axis]) for axis in range(len(dims))]
    drawn = drawn.at[tuple(spot)].set(smallest)
    longest = dims.index(max(dims))
    spot[longest] = (spot[longest] + 1) % dims[longest]
    return drawn.at[tuple(spot)].set(top_value)


def block_scale(own_key, dims, pieces, low, top_value):
    def one(dim, blocks):
        heights = jax.random.uniform(jax.random.fold_in(jax.random.fold_in(own_key, 6), dim), (blocks,), jnp.float32, low / len(pieces), top_value / len(pieces))
        return jnp.repeat(jnp.exp(heights), dims[dim] // blocks).reshape((-1,) + (1,) * (len(dims) - dim - 1))

    level = one(*pieces[0])
    for cut in pieces[1:]:
        level = level * one(*cut)
    return level


def rank_bounds(amount, lean):
    weights = [(1 << 20) // math.isqrt(standing ** lean) + 1 for standing in range(1, amount + 1)]
    deviation = 1 + sum(weights) // (1 << 30)
    return np.cumsum(np.array([max(1, weight // deviation) for weight in weights]))


def skewed_ids(rng, extent, amount, slope):
    listing = rank_bounds(amount, slope)
    pick = jax.random.randint(jax.random.fold_in(rng, 1), extent, 0, int(listing[amount - 1]))
    standing = jnp.searchsorted(jnp.asarray(listing, jnp.int32), pick, side="right")
    return jax.random.permutation(jax.random.fold_in(rng, 2), amount)[standing].astype(jnp.int32)


def noise(stream_key, dims, width, bound, cuts=(), kind=jnp.bfloat16):
    gain = block_scale(stream_key, dims, cuts, -0.22, 0.18) if cuts else 1.0
    drawn = jax.random.normal(stream_key, dims, jnp.float32) * width * gain
    return jnp.minimum(jnp.maximum(drawn, -bound), bound).astype(kind)


def setup_inputs(seed: int = 0) -> dict:
    arg_keys = jax.random.split(jax.random.key(seed), 7)
    return {
        "token_ids": touch_ends(skewed_ids(arg_keys[0], (TOKENS,), VOCAB, 2), jax.random.fold_in(arg_keys[0], 3), 0, VOCAB - 1).astype(jnp.int32),
        "embedding": draw_embedding(jax.random.fold_in(arg_keys[6], 71), 0),
        "projected": noise(arg_keys[2], (3, MIXER_CHANNELS, VOCAB), 1.0, 6.0, ((1, 8),)),
        "short_taps": noise(arg_keys[3], (TAPS, 3, MIXER_CHANNELS), TAPS ** -0.5, 2.0, ((2, 8),), jnp.float32),
        "long_filter": draw_long_filter(jax.random.fold_in(arg_keys[6], 71), 0),
        "skip_gain": noise(arg_keys[5], (MIXER_CHANNELS,), 0.5, 3.0, ((0, 8),), jnp.float32),
    }


EPSILON = 1e-06

def short_conv(padded, weights):
    tap_count = weights.shape[0]
    filter_extent = padded.shape[2] - (tap_count - 1)
    acc_sum = jnp.zeros(padded.shape[:2] + (filter_extent,), jnp.float32)
    for offset in range(tap_count):
        begin = tap_count - 1 - offset
        acc_sum = acc_sum + weights[offset][:, :, None] * padded[:, :, begin:begin + filter_extent].astype(jnp.float32)
    return acc_sum

def reference(token_ids, embedding, projected, short_taps, long_filter, skip_gain):
    values = embedding.astype(jnp.float32)
    vocab_scale = 1.0 / jnp.sqrt(lax.optimization_barrier(jnp.sum(values * values, axis=0)) / MIXER_CHANNELS + EPSILON)
    token_scale = vocab_scale[token_ids]
    block_size = math.gcd(MIXER_CHANNELS, 256)
    filter_extent = token_ids.shape[0]

    def one_block(block_index):
        channel_start = block_index * block_size
        row_slice = lax.dynamic_slice_in_dim(projected, channel_start, block_size, axis=1)
        features = (row_slice[:, :, token_ids].astype(jnp.float32) * token_scale).astype(jnp.bfloat16)
        padded = jnp.pad(features, ((0, 0), (0, 0), (TAPS - 1, 0)))
        weights = lax.dynamic_slice_in_dim(short_taps, channel_start, block_size, axis=2)
        conv_out = short_conv(padded, weights)
        gated_rows = (conv_out[1] * conv_out[2]).astype(jnp.bfloat16)
        filter_rows = lax.dynamic_slice_in_dim(long_filter, channel_start, block_size, axis=0).astype(jnp.float32)
        spectrum = jnp.fft.rfft(gated_rows.astype(jnp.float32), n=2 * filter_extent, axis=1) * jnp.fft.rfft(filter_rows, n=2 * filter_extent, axis=1)
        convolved = jnp.fft.irfft(spectrum, n=2 * filter_extent, axis=1)[:, :filter_extent]
        skip_rows = lax.dynamic_slice_in_dim(skip_gain, channel_start, block_size)
        long_out = (convolved + skip_rows[:, None] * gated_rows.astype(jnp.float32)).astype(jnp.bfloat16)
        return (conv_out[0] * long_out.astype(jnp.float32)).astype(jnp.bfloat16)
    result = lax.map(one_block, jnp.arange(MIXER_CHANNELS // block_size, dtype=jnp.int32))
    return result.reshape(MIXER_CHANNELS, filter_extent)
```

```python
import jax
import jax.numpy as jnp
import numpy as np
from jax import lax
from jax.experimental import pallas as pl
from jax.experimental.pallas import tpu as pltpu
from jax.sharding import PartitionSpec as P

MIXER_CHANNELS = 4096
EPSILON = 1e-06

LANES = 128
OUTER = 256
TOKENS = OUTER * LANES
DEVICES = 32
EIGHTHS = 8
CHANNELS = 16
VOCAB = 512
TAPS = 7
PAD = 8
BATCH = 4
ID_SHIFT = 256
CONV = 4
UX = 4
UM = 16


def transform_tables():
    place = np.arange(OUTER)
    a = (place % DEVICES) * EIGHTHS + place // DEVICES
    k1 = np.arange(OUTER)
    b = np.arange(LANES)
    outer = 2 * np.pi * ((a[:, None] * (4 * k1[None, :] + 1)) % 1024) / 1024
    forward = np.concatenate([np.cos(outer), -np.sin(outer)], axis=1)
    backward = np.concatenate([np.cos(outer).T, -np.sin(outer).T], axis=0) / TOKENS
    twist = 2 * np.pi * (b[:, None] * (4 * k1[None, :] + 1)) / (4 * TOKENS)
    inner = 2 * np.pi * ((b[:, None] * b[None, :]) % LANES) / LANES
    cos, sin = np.cos(inner), np.sin(inner)
    inward = np.block([[cos, sin], [-sin, cos]])
    outward = np.block([[cos, -sin], [sin, cos]])
    half = lambda x: jnp.asarray(x.astype(np.float32)).astype(jnp.bfloat16)
    full = lambda x: jnp.asarray(x.astype(np.float32))
    return (
        half(forward),
        full(np.stack([np.cos(twist), np.sin(twist)])),
        half(inward),
        half(outward),
        half(backward),
    )


def pick_lanes(table, lanes):
    numbers = lax.GatherDimensionNumbers(
        offset_dims=(), collapsed_slice_dims=(1,), start_index_map=(1,),
        operand_batching_dims=(0,), start_indices_batching_dims=(0,),
    )
    return lax.gather(
        table, lanes[..., None], numbers, slice_sizes=(1, 1), mode=lax.GatherScatterMode.PROMISE_IN_BOUNDS
    )


def every(ref, first, count, step):
    return ref[pl.ds(first, count, stride=step), :]


def both_sides(ref, channel):
    return jnp.concatenate([every(ref.at[side], channel, LANES, CHANNELS) for side in range(2)], axis=1)


def mixer_kernel(
    skip_ref, mail_ref, table_ref, taps_ref, forward_hbm, twist_hbm, inward_hbm, outward_hbm, backward_hbm,
    out_ref,
    ids, ids_t, features, first, gated, taps, result, x_hat, h_hat,
    forward, twist, inward, outward, backward, sems,
):
    f32, bf16 = jnp.float32, jnp.bfloat16
    copies = [
        pltpu.make_async_copy(source, target, sems.at[i])
        for i, (source, target) in enumerate((
            (forward_hbm, forward), (twist_hbm, twist), (inward_hbm, inward),
            (outward_hbm, outward), (backward_hbm, backward),
        ))
    ]
    for copy in copies:
        copy.start()
    lane = lax.broadcasted_iota(jnp.int32, (CHANNELS, LANES), 1)

    for d in range(DEVICES):
        ids[d * EIGHTHS : (d + 1) * EIGHTHS] = mail_ref[d, :, 2 * EIGHTHS * LANES :].astype(f32)
    turned_ids = jnp.concatenate([every(ids, e, DEVICES, EIGHTHS) for e in range(EIGHTHS)], axis=0).T
    for side in range(2):
        ids_t[side] = turned_ids[:, side * LANES : (side + 1) * LANES].astype(jnp.int32) + ID_SHIFT

    def unpack(d, carry):
        for half in range(2):
            row = pl.multiple_of(d * CHANNELS + half * 8, 8)
            for e in range(EIGHTHS):
                column = (half * EIGHTHS + e) * LANES
                taps[e, pl.ds(row, 8), :] = mail_ref[d, :, column : column + LANES].astype(f32)
        return carry

    lax.fori_loop(0, DEVICES, unpack, 0, unroll=4)
    for copy in copies:
        copy.wait()

    def look_up(b):
        for side in range(2):
            token = jnp.broadcast_to(ids_t[side, pl.ds(b, 1), :], (CHANNELS, LANES))
            low = (token & (LANES - 1)).astype(jnp.int16)
            token = token.astype(jnp.int16)
            odd = (token & LANES) != 0
            upper = (token & (2 * LANES)) != 0
            for j in range(3):
                picks = [pick_lanes(table_ref[j, :, q * LANES : (q + 1) * LANES], low) for q in range(4)]
                features[j * 2 + side, b + PAD] = jnp.where(
                    upper, jnp.where(odd, picks[3], picks[2]), jnp.where(odd, picks[1], picks[0])
                )

    def transform(signals, store, start):
        z = jnp.dot(jnp.concatenate(signals, axis=0), forward[...], preferred_element_type=f32)
        cos, sin = twist[0], twist[1]
        for i in range(len(signals)):
            real, imag = z[i * LANES : (i + 1) * LANES, :OUTER], z[i * LANES : (i + 1) * LANES, OUTER:]
            turned = jnp.concatenate([real * cos + imag * sin, imag * cos - real * sin], axis=0)
            store[start + i] = jnp.dot(inward[...], turned.astype(bf16), preferred_element_type=f32).astype(
                store.dtype
            )

    def filters_of(start):
        transform(
            [
                jnp.concatenate(
                    [every(taps.at[e], start + i, DEVICES, CHANNELS) for e in range(EIGHTHS)], axis=0
                ).T.astype(bf16)
                for i in range(BATCH)
            ],
            h_hat, start,
        )

    def look_and_filter(block, carry):
        filters_of(block * BATCH)
        for i in range(LANES * BATCH // CHANNELS):
            look_up(block * (LANES * BATCH // CHANNELS) + i)
        return carry

    lax.fori_loop(0, CHANNELS // BATCH, look_and_filter, 0)

    for j in range(3):
        for back in range(1, TAPS):
            left = features[2 * j, PAD + LANES - back].astype(f32)
            right = features[2 * j + 1, PAD + LANES - back].astype(f32)
            by_32 = pltpu.roll(left, 32, 1)
            wrapped = jnp.where(lane == 0, 0.0, pltpu.roll(right, 33, 1))
            features[2 * j, PAD - back] = jnp.where(lane < 32, wrapped, by_32).astype(bf16)
            features[2 * j + 1, PAD - back] = jnp.where(lane < 32, by_32, pltpu.roll(right, 32, 1)).astype(bf16)

    def convolve(block, carry):
        start = block * CONV
        for side in range(2):
            sums = []
            for j in range(3):
                window = [
                    features[j * 2 + side, start + PAD - (TAPS - 1) + i].astype(f32)
                    for i in range(CONV + TAPS - 1)
                ]
                out = []
                for i in range(CONV):
                    total = taps_ref[j] * window[i + TAPS - 1]
                    for k in range(1, TAPS):
                        total = total + taps_ref[k * 3 + j] * window[i + TAPS - 1 - k]
                    out.append(total)
                sums.append(out)
            for i in range(CONV):
                row = pl.ds(pl.multiple_of((start + i) * CHANNELS, CHANNELS), CHANNELS)
                first[side, row, :] = sums[0][i]
                gated[side, row, :] = (sums[1][i] * sums[2][i]).astype(bf16).astype(f32)
        return carry

    lax.fori_loop(0, LANES // CONV, convolve, 0)

    def streams_of(block, carry):
        start = block * BATCH
        transform([both_sides(gated, start + i).astype(bf16) for i in range(BATCH)], x_hat, start)
        return carry

    lax.fori_loop(0, CHANNELS // BATCH, streams_of, 0, unroll=UX)

    def mix(c, carry):
        h_real, h_imag = h_hat[c, :LANES], h_hat[c, LANES:]
        x_real, x_imag = x_hat[c, :LANES].astype(f32), x_hat[c, LANES:].astype(f32)
        product = jnp.concatenate(
            [x_real * h_real - x_imag * h_imag, x_real * h_imag + x_imag * h_real], axis=0
        )
        p = jnp.dot(outward[...], product.astype(bf16), preferred_element_type=f32)
        real, imag = p[:LANES], p[LANES:]
        cos, sin = twist[0], twist[1]
        q = jnp.concatenate([real * cos - imag * sin, imag * cos + real * sin], axis=1)
        y = jnp.dot(q.astype(bf16), backward[...], preferred_element_type=f32)
        long_out = (y + skip_ref[c] * both_sides(gated, c)).astype(bf16).astype(f32)
        mixed = (both_sides(first, c) * long_out).T
        for e in range(EIGHTHS):
            result[e, pl.ds(c, DEVICES, stride=CHANNELS), :] = mixed[e * DEVICES : (e + 1) * DEVICES]
        return carry

    lax.fori_loop(0, CHANNELS, mix, 0, unroll=UM)
    for e in range(EIGHTHS):
        out_ref[:, e * LANES : (e + 1) * LANES] = result[e].astype(bf16)


def mix_tokens(skip, mail, table, taps):
    whole = pl.BlockSpec(memory_space=pltpu.VMEM)
    outside = pl.BlockSpec(memory_space=pl.ANY)
    bf16, f32 = jnp.bfloat16, jnp.float32
    tables = transform_tables()
    return pl.pallas_call(
        mixer_kernel,
        out_shape=jax.ShapeDtypeStruct((DEVICES * CHANNELS, EIGHTHS * LANES), bf16),
        in_specs=[pl.BlockSpec(memory_space=pltpu.SMEM), whole, whole, whole] + [outside] * len(tables),
        out_specs=whole,
        scratch_shapes=[
            pltpu.VMEM((OUTER, LANES), f32),
            pltpu.VMEM((2, LANES, LANES), jnp.int32),
            pltpu.VMEM((6, PAD + LANES, CHANNELS, LANES), bf16),
            pltpu.VMEM((2, LANES * CHANNELS, LANES), f32),
            pltpu.VMEM((2, LANES * CHANNELS, LANES), f32),
            pltpu.VMEM((EIGHTHS, DEVICES * CHANNELS, LANES), f32),
            pltpu.VMEM((EIGHTHS, DEVICES * CHANNELS, LANES), f32),
            pltpu.VMEM((CHANNELS, 2 * LANES, OUTER), bf16),
            pltpu.VMEM((CHANNELS, 2 * LANES, OUTER), f32),
        ]
        + [pltpu.VMEM(table.shape, table.dtype) for table in tables]
        + [pltpu.SemaphoreType.DMA((len(tables),))],
        compiler_params=pltpu.CompilerParams(vmem_limit_bytes=44 * 2**20),
        cost_estimate=pl.CostEstimate(flops=4 * 10**9, bytes_accessed=4 * 10**6, transcendentals=0),
        name="mixer",
    )(skip, mail, table, taps, *tables)


def ring_sum(value, axis):
    size = lax.axis_size(axis)
    assert size == 8

    def arriving_from(x, by):
        return lax.ppermute(x, axis, [((i + by) % size, i) for i in range(size)])

    after = arriving_from(value, 1)
    before = arriving_from(value, -1)
    pair = value + after
    three = pair + before
    return three + arriving_from(three, 3) + arriving_from(pair, -3)


def shards(token_ids, embedding, projected, short_taps, long_filter, skip_gain):
    rank = lax.axis_index("seq")

    filters = long_filter.reshape(DEVICES, 2, 8, EIGHTHS * LANES)
    ids = (token_ids - ID_SHIFT).astype(jnp.bfloat16).reshape(1, EIGHTHS, LANES)
    letters = jnp.concatenate(
        [filters[:, 0], filters[:, 1], jnp.broadcast_to(ids, (DEVICES, EIGHTHS, LANES))], axis=2
    )
    mail = lax.all_to_all(letters, "seq", split_axis=0, concat_axis=0, tiled=True)

    values = embedding.astype(jnp.float32)
    squares = ring_sum(jnp.sum(values * values, axis=0, keepdims=True), "ch")
    scale = 1.0 / jnp.sqrt(squares / MIXER_CHANNELS + EPSILON)
    own = lax.dynamic_slice_in_dim(projected, rank * CHANNELS, CHANNELS, axis=1)
    table = (own.astype(jnp.float32) * scale[None]).astype(jnp.bfloat16)

    own_taps = lax.dynamic_slice_in_dim(short_taps, rank * CHANNELS, CHANNELS, axis=2)
    taps = jnp.broadcast_to(own_taps.reshape(TAPS * 3, CHANNELS, 1), (TAPS * 3, CHANNELS, LANES))
    skip = lax.dynamic_slice_in_dim(skip_gain, rank * CHANNELS, CHANNELS)

    mixed = mix_tokens(skip, mail, table, taps)
    return lax.all_to_all(mixed, "seq", split_axis=0, concat_axis=0, tiled=True)


def solution(mesh):
    placed = (
        P("seq"),
        P("ch", None),
        P(None, "ch", None),
        P(None, None, "ch"),
        P("ch", "seq"),
        P("ch"),
    )
    return jax.shard_map(shards, mesh=mesh, in_specs=placed, out_specs=P("ch", "seq"), check_vma=False)
```

```python
import jax
import jax.numpy as jnp
import numpy as np
from jax import lax
from jax.experimental import pallas as pl
from jax.experimental.pallas import tpu as pltpu
from jax.sharding import PartitionSpec as P

MIXER_CHANNELS = 4096
EPSILON = 1e-06

LANES = 128
OUTER = 256
TOKENS = OUTER * LANES
DEVICES = 32
EIGHTHS = 8
CHANNELS = 16
VOCAB = 512
TAPS = 7
PAD = 8
BATCH = 4
ID_SHIFT = 256
STEP = 8
CONV = 4
SHARE = 16


def transform_tables():
    place = np.arange(OUTER)
    a = (place % DEVICES) * EIGHTHS + place // DEVICES
    k1 = np.arange(OUTER)
    b = np.arange(LANES)
    outer = 2 * np.pi * ((a[:, None] * (4 * k1[None, :] + 1)) % 1024) / 1024
    forward = np.concatenate([np.cos(outer), -np.sin(outer)], axis=1)
    backward = np.concatenate([np.cos(outer).T, -np.sin(outer).T], axis=0) / TOKENS
    twist = 2 * np.pi * (b[:, None] * (4 * k1[None, :] + 1)) / (4 * TOKENS)
    inner = 2 * np.pi * ((b[:, None] * b[None, :]) % LANES) / LANES
    cos, sin = np.cos(inner), np.sin(inner)
    inward = np.block([[cos, sin], [-sin, cos]])
    outward = np.block([[cos, -sin], [sin, cos]])
    half = lambda x: jnp.asarray(x.astype(np.float32)).astype(jnp.bfloat16)
    full = lambda x: jnp.asarray(x.astype(np.float32))
    return (
        half(forward),
        full(np.stack([np.cos(twist), np.sin(twist)])),
        half(inward),
        half(outward),
        half(backward),
    )


def pick_lanes(table, lanes):
    numbers = lax.GatherDimensionNumbers(
        offset_dims=(), collapsed_slice_dims=(1,), start_index_map=(1,),
        operand_batching_dims=(0,), start_indices_batching_dims=(0,),
    )
    return lax.gather(
        table, lanes[..., None], numbers, slice_sizes=(1, 1), mode=lax.GatherScatterMode.PROMISE_IN_BOUNDS
    )


def every(ref, first, count, step):
    return ref[pl.ds(first, count, stride=step), :]


def both_sides(ref, channel):
    return jnp.concatenate([every(ref.at[side], channel, LANES, CHANNELS) for side in range(2)], axis=1)


def mixer_kernel(
    skip_ref, mail_ref, table_ref, taps_ref, forward_hbm, twist_hbm, inward_hbm, outward_hbm, backward_hbm,
    out_ref,
    ids, ids_t, features, first, gated, taps, result, h_hat,
    forward, twist, inward, outward, backward, sems,
):
    f32, bf16 = jnp.float32, jnp.bfloat16
    copies = [
        pltpu.make_async_copy(source, target, sems.at[i])
        for i, (source, target) in enumerate((
            (forward_hbm, forward), (twist_hbm, twist), (inward_hbm, inward),
            (outward_hbm, outward), (backward_hbm, backward),
        ))
    ]
    for copy in copies:
        copy.start()
    lane = lax.broadcasted_iota(jnp.int32, (CHANNELS, LANES), 1)

    for d in range(DEVICES):
        ids[d * EIGHTHS : (d + 1) * EIGHTHS] = mail_ref[d, :, 2 * EIGHTHS * LANES :].astype(f32)
    turned_ids = jnp.concatenate([every(ids, e, DEVICES, EIGHTHS) for e in range(EIGHTHS)], axis=0).T
    for side in range(2):
        ids_t[side] = turned_ids[:, side * LANES : (side + 1) * LANES].astype(jnp.int32) + ID_SHIFT

    def unpack(d, carry):
        for half in range(2):
            row = pl.multiple_of(d * CHANNELS + half * 8, 8)
            for e in range(EIGHTHS):
                column = (half * EIGHTHS + e) * LANES
                taps[e, pl.ds(row, 8), :] = mail_ref[d, :, column : column + LANES].astype(f32)
        return carry

    lax.fori_loop(0, DEVICES, unpack, 0, unroll=4)
    def look_up(b):
        for side in range(2):
            token = jnp.broadcast_to(ids_t[side, pl.ds(b, 1), :], (CHANNELS, LANES))
            low = (token & (LANES - 1)).astype(jnp.int16)
            token = token.astype(jnp.int16)
            odd = (token & LANES) != 0
            upper = (token & (2 * LANES)) != 0
            for j in range(3):
                picks = [pick_lanes(table_ref[j, :, q * LANES : (q + 1) * LANES], low) for q in range(4)]
                features[j * 2 + side, b + PAD] = jnp.where(
                    upper, jnp.where(odd, picks[3], picks[2]), jnp.where(odd, picks[1], picks[0])
                ).astype(f32)

    def transform(signals):
        z = jnp.dot(jnp.concatenate(signals, axis=0), forward[...], preferred_element_type=f32)
        cos, sin = twist[0], twist[1]
        out = []
        for i in range(len(signals)):
            real, imag = z[i * LANES : (i + 1) * LANES, :OUTER], z[i * LANES : (i + 1) * LANES, OUTER:]
            turned = jnp.concatenate([real * cos + imag * sin, imag * cos - real * sin], axis=0)
            out.append(jnp.dot(inward[...], turned.astype(bf16), preferred_element_type=f32))
        return out

    def transform_filters(start, count):
        found = transform([
            jnp.concatenate([every(taps.at[e], start + i, DEVICES, CHANNELS) for e in range(EIGHTHS)], axis=0)
            .T.astype(bf16)
            for i in range(count)
        ])
        for i, value in enumerate(found):
            h_hat[start + i, :LANES] = value[:LANES] + skip_ref[start + i]
            h_hat[start + i, LANES:] = value[LANES:]

    def carry_over():
        for j in range(3):
            for back in range(1, TAPS):
                left = features[2 * j, PAD + LANES - back]
                right = features[2 * j + 1, PAD + LANES - back]
                by_32 = pltpu.roll(left, 32, 1)
                wrapped = jnp.where(lane == 0, 0.0, pltpu.roll(right, 33, 1))
                features[2 * j, PAD - back] = jnp.where(lane < 32, wrapped, by_32)
                features[2 * j + 1, PAD - back] = jnp.where(lane < 32, by_32, pltpu.roll(right, 32, 1))

    def convolve(start):
        for side in range(2):
            sums = []
            for j in range(3):
                window = [
                    features[j * 2 + side, start + PAD - (TAPS - 1) + i] for i in range(CONV + TAPS - 1)
                ]
                out = []
                for i in range(CONV):
                    total = taps_ref[j] * window[i + TAPS - 1]
                    for k in range(1, TAPS):
                        total = total + taps_ref[k * 3 + j] * window[i + TAPS - 1 - k]
                    out.append(total)
                sums.append(out)
            for i in range(CONV):
                row = pl.ds((start + i) * CHANNELS, CHANNELS)
                first[side, row, :] = sums[0][i]
                gated[side, row, :] = (sums[1][i] * sums[2][i]).astype(bf16).astype(f32)

    steps = LANES // STEP
    for i in range(STEP):
        look_up(LANES - STEP + i)
    carry_over()
    for i in range(STEP):
        look_up(i)
    for copy in copies:
        copy.wait()
    for block in range(steps):
        if block + 1 < steps - 1:
            for i in range(STEP):
                look_up((block + 1) * STEP + i)
        transform_filters(block * CHANNELS // steps, CHANNELS // steps)
        for i in range(0, STEP, CONV):
            convolve(block * STEP + i)

    for start in range(0, CHANNELS, BATCH):
        streams = transform([both_sides(gated, start + i).astype(bf16) for i in range(BATCH)])
        turned = []
        for i in range(BATCH):
            h_real, h_imag = h_hat[start + i, :LANES], h_hat[start + i, LANES:]
            x_real, x_imag = streams[i][:LANES], streams[i][LANES:]
            product = jnp.concatenate(
                [x_real * h_real - x_imag * h_imag, x_real * h_imag + x_imag * h_real], axis=0
            )
            p = jnp.dot(outward[...], product.astype(bf16), preferred_element_type=f32)
            real, imag = p[:LANES], p[LANES:]
            cos, sin = twist[0], twist[1]
            turned.append(
                jnp.concatenate([real * cos - imag * sin, imag * cos + real * sin], axis=1).astype(bf16)
            )
        long_out = jnp.dot(jnp.concatenate(turned, axis=0), backward[...], preferred_element_type=f32)
        for i in range(BATCH):
            rounded = long_out[i * LANES : (i + 1) * LANES].astype(bf16).astype(f32)
            mixed = (both_sides(first, start + i) * rounded).T
            for e in range(EIGHTHS):
                result[e, pl.ds(start + i, DEVICES, stride=CHANNELS), :] = mixed[e * DEVICES : (e + 1) * DEVICES]
    for e in range(EIGHTHS):
        out_ref[:, e * LANES : (e + 1) * LANES] = result[e].astype(bf16)


def mix_tokens(skip, mail, table, taps):
    whole = pl.BlockSpec(memory_space=pltpu.VMEM)
    outside = pl.BlockSpec(memory_space=pl.ANY)
    bf16, f32 = jnp.bfloat16, jnp.float32
    tables = transform_tables()
    return pl.pallas_call(
        mixer_kernel,
        out_shape=jax.ShapeDtypeStruct((DEVICES * CHANNELS, EIGHTHS * LANES), bf16),
        in_specs=[pl.BlockSpec(memory_space=pltpu.SMEM), whole, whole, whole] + [outside] * len(tables),
        out_specs=whole,
        scratch_shapes=[
            pltpu.VMEM((OUTER, LANES), f32),
            pltpu.VMEM((2, LANES, LANES), jnp.int32),
            pltpu.VMEM((6, PAD + LANES, CHANNELS, LANES), f32),
            pltpu.VMEM((2, LANES * CHANNELS, LANES), f32),
            pltpu.VMEM((2, LANES * CHANNELS, LANES), f32),
            pltpu.VMEM((EIGHTHS, DEVICES * CHANNELS, LANES), f32),
            pltpu.VMEM((EIGHTHS, DEVICES * CHANNELS, LANES), f32),
            pltpu.VMEM((CHANNELS, 2 * LANES, OUTER), f32),
        ]
        + [pltpu.VMEM(table.shape, table.dtype) for table in tables]
        + [pltpu.SemaphoreType.DMA((len(tables),))],
        compiler_params=pltpu.CompilerParams(vmem_limit_bytes=44 * 2**20),
        cost_estimate=pl.CostEstimate(flops=4 * 10**9, bytes_accessed=4 * 10**6, transcendentals=0),
        name="mixer",
    )(skip, mail, table, taps, *tables)


def letters_kernel(filter_ref, ids_ref, out_ref):
    width = EIGHTHS * LANES
    for half in range(2):
        out_ref[:, :, half * width : (half + 1) * width] = filter_ref[:, half]
    ids = (ids_ref[...] - ID_SHIFT).astype(jnp.float32).astype(jnp.bfloat16)
    out_ref[:, :, 2 * width :] = jnp.broadcast_to(ids[None], (out_ref.shape[0], EIGHTHS, LANES))


def write_letters(filters, ids):
    width = EIGHTHS * LANES
    return pl.pallas_call(
        letters_kernel,
        out_shape=jax.ShapeDtypeStruct((DEVICES, 8, 2 * width + LANES), jnp.bfloat16),
        grid=(DEVICES // SHARE,),
        in_specs=[
            pl.BlockSpec((SHARE, 2, 8, width), lambda i: (i, 0, 0, 0)),
            pl.BlockSpec((EIGHTHS, LANES), lambda i: (0, 0)),
        ],
        out_specs=pl.BlockSpec((SHARE, 8, 2 * width + LANES), lambda i: (i, 0, 0)),
        cost_estimate=pl.CostEstimate(flops=0, bytes_accessed=2 * 2**20, transcendentals=0),
        name="letters",
    )(filters, ids)


def ring_sum(value, axis):
    size = lax.axis_size(axis)
    assert size == 8

    def arriving_from(x, by):
        return lax.ppermute(x, axis, [((i + by) % size, i) for i in range(size)])

    after = arriving_from(value, 1)
    before = arriving_from(value, -1)
    pair = value + after
    three = pair + before
    return three + arriving_from(three, 3) + arriving_from(pair, -3)


def shards(token_ids, embedding, projected, short_taps, long_filter, skip_gain):
    rank = lax.axis_index("seq")

    values = embedding.astype(jnp.float32)
    partial = jnp.sum(values * values, axis=0, keepdims=True)
    squares = ring_sum(partial, "ch")
    letters = write_letters(
        long_filter.reshape(DEVICES, 2, 8, EIGHTHS * LANES), token_ids.reshape(EIGHTHS, LANES)
    )
    mail = lax.all_to_all(letters, "seq", split_axis=0, concat_axis=0, tiled=True)

    scale = 1.0 / jnp.sqrt(squares / MIXER_CHANNELS + EPSILON)
    own = lax.dynamic_slice_in_dim(projected, rank * CHANNELS, CHANNELS, axis=1)
    table = (own.astype(jnp.float32) * scale[None]).astype(jnp.bfloat16)

    own_taps = lax.dynamic_slice_in_dim(short_taps, rank * CHANNELS, CHANNELS, axis=2)
    taps = jnp.broadcast_to(own_taps.reshape(TAPS * 3, CHANNELS, 1), (TAPS * 3, CHANNELS, LANES))
    skip = lax.dynamic_slice_in_dim(skip_gain, rank * CHANNELS, CHANNELS)

    mixed = mix_tokens(skip, mail, table, taps)
    return lax.all_to_all(mixed, "seq", split_axis=0, concat_axis=0, tiled=True)


def solution(mesh):
    placed = (
        P("seq"),
        P("ch", None),
        P(None, "ch", None),
        P(None, None, "ch"),
        P("ch", "seq"),
        P("ch"),
    )
    return jax.shard_map(shards, mesh=mesh, in_specs=placed, out_specs=P("ch", "seq"), check_vma=False)
```

```python
import jax
import jax.numpy as jnp
import numpy as np
from jax import lax
from jax.experimental import pallas as pl
from jax.experimental.pallas import tpu as pltpu
from jax.sharding import PartitionSpec as P

MIXER_CHANNELS = 4096
EPSILON = 1e-06

LANES = 128
OUTER = 256
TOKENS = OUTER * LANES
DEVICES = 32
EIGHTHS = 8
CHANNELS = 16
VOCAB = 512
TAPS = 7
PAD = 8
BATCH = 4
ID_SHIFT = 256
STEP = 8
CONV = 4
SHARE = 16


def transform_tables():
    place = np.arange(OUTER)
    a = (place % DEVICES) * EIGHTHS + place // DEVICES
    k1 = np.arange(OUTER)
    b = np.arange(LANES)
    outer = 2 * np.pi * ((a[:, None] * (4 * k1[None, :] + 1)) % 1024) / 1024
    forward = np.concatenate([np.cos(outer), -np.sin(outer)], axis=1)
    backward = np.concatenate([np.cos(outer).T, -np.sin(outer).T], axis=0) / TOKENS
    twist = 2 * np.pi * (b[:, None] * (4 * k1[None, :] + 1)) / (4 * TOKENS)
    inner = 2 * np.pi * ((b[:, None] * b[None, :]) % LANES) / LANES
    cos, sin = np.cos(inner), np.sin(inner)
    inward = np.block([[cos, sin], [-sin, cos]])
    outward = np.block([[cos, -sin], [sin, cos]])
    half = lambda x: jnp.asarray(x.astype(np.float32)).astype(jnp.bfloat16)
    full = lambda x: jnp.asarray(x.astype(np.float32))
    return (
        half(forward),
        full(np.stack([np.cos(twist), np.sin(twist)])),
        half(inward),
        half(outward),
        half(backward),
    )


def pick_lanes(table, lanes):
    numbers = lax.GatherDimensionNumbers(
        offset_dims=(), collapsed_slice_dims=(1,), start_index_map=(1,),
        operand_batching_dims=(0,), start_indices_batching_dims=(0,),
    )
    return lax.gather(
        table, lanes[..., None], numbers, slice_sizes=(1, 1), mode=lax.GatherScatterMode.PROMISE_IN_BOUNDS
    )


def every(ref, first, count, step):
    return ref[pl.ds(first, count, stride=step), :]


def both_sides(ref, channel):
    return jnp.concatenate([every(ref.at[side], channel, LANES, CHANNELS) for side in range(2)], axis=1)


def mixer_kernel(
    skip_ref, mail_ref, table_ref, taps_ref, forward_hbm, twist_hbm, inward_hbm, outward_hbm, backward_hbm,
    out_ref,
    ids, ids_t, features, first, gated, taps, result, h_hat,
    forward, twist, inward, outward, backward, sems,
):
    f32, bf16 = jnp.float32, jnp.bfloat16
    copies = [
        pltpu.make_async_copy(source, target, sems.at[i])
        for i, (source, target) in enumerate((
            (forward_hbm, forward), (twist_hbm, twist), (inward_hbm, inward),
            (outward_hbm, outward), (backward_hbm, backward),
        ))
    ]
    for copy in copies:
        copy.start()
    lane = lax.broadcasted_iota(jnp.int32, (CHANNELS, LANES), 1)

    for d in range(DEVICES):
        ids[d * EIGHTHS : (d + 1) * EIGHTHS] = mail_ref[d, :, 2 * EIGHTHS * LANES :].astype(f32)
    turned_ids = jnp.concatenate([every(ids, e, DEVICES, EIGHTHS) for e in range(EIGHTHS)], axis=0).T
    for side in range(2):
        ids_t[side] = turned_ids[:, side * LANES : (side + 1) * LANES].astype(jnp.int32) + ID_SHIFT

    def unpack(d, carry):
        for half in range(2):
            row = pl.multiple_of(d * CHANNELS + half * 8, 8)
            for e in range(EIGHTHS):
                column = (half * EIGHTHS + e) * LANES
                taps[e, pl.ds(row, 8), :] = mail_ref[d, :, column : column + LANES].astype(f32)
        return carry

    lax.fori_loop(0, DEVICES, unpack, 0, unroll=4)
    def look_up(b):
        for side in range(2):
            token = jnp.broadcast_to(ids_t[side, pl.ds(b, 1), :], (CHANNELS, LANES))
            low = (token & (LANES - 1)).astype(jnp.int16)
            token = token.astype(jnp.int16)
            odd = (token & LANES) != 0
            upper = (token & (2 * LANES)) != 0
            for j in range(3):
                picks = [pick_lanes(table_ref[j, :, q * LANES : (q + 1) * LANES], low) for q in range(4)]
                features[j * 2 + side, b + PAD] = jnp.where(
                    upper, jnp.where(odd, picks[3], picks[2]), jnp.where(odd, picks[1], picks[0])
                ).astype(f32)

    def transform(signals):
        z = jnp.dot(jnp.concatenate(signals, axis=0), forward[...], preferred_element_type=f32)
        cos, sin = twist[0], twist[1]
        out = []
        for i in range(len(signals)):
            real, imag = z[i * LANES : (i + 1) * LANES, :OUTER], z[i * LANES : (i + 1) * LANES, OUTER:]
            turned = jnp.concatenate([real * cos + imag * sin, imag * cos - real * sin], axis=0)
            out.append(jnp.dot(inward[...], turned.astype(bf16), preferred_element_type=f32))
        return out

    def transform_filters(start, count):
        found = transform([
            jnp.concatenate([every(taps.at[e], start + i, DEVICES, CHANNELS) for e in range(EIGHTHS)], axis=0)
            .T.astype(bf16)
            for i in range(count)
        ])
        for i, value in enumerate(found):
            h_hat[start + i, :LANES] = value[:LANES] + skip_ref[start + i]
            h_hat[start + i, LANES:] = value[LANES:]

    def carry_over():
        for j in range(3):
            for back in range(1, TAPS):
                left = features[2 * j, PAD + LANES - back]
                right = features[2 * j + 1, PAD + LANES - back]
                by_32 = pltpu.roll(left, 32, 1)
                wrapped = jnp.where(lane == 0, 0.0, pltpu.roll(right, 33, 1))
                features[2 * j, PAD - back] = jnp.where(lane < 32, wrapped, by_32)
                features[2 * j + 1, PAD - back] = jnp.where(lane < 32, by_32, pltpu.roll(right, 32, 1))

    def convolve(start):
        for side in range(2):
            sums = []
            for j in range(3):
                window = [
                    features[j * 2 + side, start + PAD - (TAPS - 1) + i] for i in range(CONV + TAPS - 1)
                ]
                out = []
                for i in range(CONV):
                    total = taps_ref[j] * window[i + TAPS - 1]
                    for k in range(1, TAPS):
                        total = total + taps_ref[k * 3 + j] * window[i + TAPS - 1 - k]
                    out.append(total)
                sums.append(out)
            for i in range(CONV):
                row = pl.ds((start + i) * CHANNELS, CHANNELS)
                first[side, row, :] = sums[0][i]
                gated[side, row, :] = (sums[1][i] * sums[2][i]).astype(bf16).astype(f32)

    steps = LANES // STEP
    for i in range(STEP):
        look_up(LANES - STEP + i)
    carry_over()
    for i in range(STEP):
        look_up(i)
    for copy in copies:
        copy.wait()
    for block in range(steps):
        if block + 1 < steps - 1:
            for i in range(STEP):
                look_up((block + 1) * STEP + i)
        transform_filters(block * CHANNELS // steps, CHANNELS // steps)
        for i in range(0, STEP, CONV):
            convolve(block * STEP + i)

    def transform_streams(start):
        return transform([both_sides(gated, start + i).astype(bf16) for i in range(BATCH)])

    following = transform_streams(0)
    for start in range(0, CHANNELS, BATCH):
        streams = following
        if start + BATCH < CHANNELS:
            following = transform_streams(start + BATCH)
        turned = []
        for i in range(BATCH):
            h_real, h_imag = h_hat[start + i, :LANES], h_hat[start + i, LANES:]
            x_real, x_imag = streams[i][:LANES], streams[i][LANES:]
            product = jnp.concatenate(
                [x_real * h_real - x_imag * h_imag, x_real * h_imag + x_imag * h_real], axis=0
            )
            p = jnp.dot(outward[...], product.astype(bf16), preferred_element_type=f32)
            real, imag = p[:LANES], p[LANES:]
            cos, sin = twist[0], twist[1]
            turned.append(
                jnp.concatenate([real * cos - imag * sin, imag * cos + real * sin], axis=1).astype(bf16)
            )
        long_out = jnp.dot(jnp.concatenate(turned, axis=0), backward[...], preferred_element_type=f32)
        for i in range(BATCH):
            rounded = long_out[i * LANES : (i + 1) * LANES].astype(bf16).astype(f32)
            mixed = (both_sides(first, start + i) * rounded).T
            for e in range(EIGHTHS):
                result[e, pl.ds(start + i, DEVICES, stride=CHANNELS), :] = mixed[e * DEVICES : (e + 1) * DEVICES]
    for e in range(EIGHTHS):
        out_ref[:, e * LANES : (e + 1) * LANES] = result[e].astype(bf16)


def mix_tokens(skip, mail, table, taps):
    whole = pl.BlockSpec(memory_space=pltpu.VMEM)
    outside = pl.BlockSpec(memory_space=pl.ANY)
    bf16, f32 = jnp.bfloat16, jnp.float32
    tables = transform_tables()
    return pl.pallas_call(
        mixer_kernel,
        out_shape=jax.ShapeDtypeStruct((DEVICES * CHANNELS, EIGHTHS * LANES), bf16),
        in_specs=[pl.BlockSpec(memory_space=pltpu.SMEM), whole, whole, whole] + [outside] * len(tables),
        out_specs=whole,
        scratch_shapes=[
            pltpu.VMEM((OUTER, LANES), f32),
            pltpu.VMEM((2, LANES, LANES), jnp.int32),
            pltpu.VMEM((6, PAD + LANES, CHANNELS, LANES), f32),
            pltpu.VMEM((2, LANES * CHANNELS, LANES), f32),
            pltpu.VMEM((2, LANES * CHANNELS, LANES), f32),
            pltpu.VMEM((EIGHTHS, DEVICES * CHANNELS, LANES), f32),
            pltpu.VMEM((EIGHTHS, DEVICES * CHANNELS, LANES), f32),
            pltpu.VMEM((CHANNELS, 2 * LANES, OUTER), f32),
        ]
        + [pltpu.VMEM(table.shape, table.dtype) for table in tables]
        + [pltpu.SemaphoreType.DMA((len(tables),))],
        compiler_params=pltpu.CompilerParams(vmem_limit_bytes=44 * 2**20),
        cost_estimate=pl.CostEstimate(flops=4 * 10**9, bytes_accessed=4 * 10**6, transcendentals=0),
        name="mixer",
    )(skip, mail, table, taps, *tables)


def letters_kernel(filter_ref, ids_ref, out_ref):
    width = EIGHTHS * LANES
    for half in range(2):
        out_ref[:, :, half * width : (half + 1) * width] = filter_ref[:, half]
    ids = (ids_ref[...] - ID_SHIFT).astype(jnp.float32).astype(jnp.bfloat16)
    out_ref[:, :, 2 * width :] = jnp.broadcast_to(ids[None], (out_ref.shape[0], EIGHTHS, LANES))


def write_letters(filters, ids):
    width = EIGHTHS * LANES
    return pl.pallas_call(
        letters_kernel,
        out_shape=jax.ShapeDtypeStruct((DEVICES, 8, 2 * width + LANES), jnp.bfloat16),
        grid=(DEVICES // SHARE,),
        in_specs=[
            pl.BlockSpec((SHARE, 2, 8, width), lambda i: (i, 0, 0, 0)),
            pl.BlockSpec((EIGHTHS, LANES), lambda i: (0, 0)),
        ],
        out_specs=pl.BlockSpec((SHARE, 8, 2 * width + LANES), lambda i: (i, 0, 0)),
        cost_estimate=pl.CostEstimate(flops=0, bytes_accessed=2 * 2**20, transcendentals=0),
        name="letters",
    )(filters, ids)


def ring_sum(value, axis):
    size = lax.axis_size(axis)
    assert size == 8

    def arriving_from(x, by):
        return lax.ppermute(x, axis, [((i + by) % size, i) for i in range(size)])

    after = arriving_from(value, 1)
    before = arriving_from(value, -1)
    pair = value + after
    three = pair + before
    return three + arriving_from(three, 3) + arriving_from(pair, -3)


def shards(token_ids, embedding, projected, short_taps, long_filter, skip_gain):
    rank = lax.axis_index("seq")

    values = embedding.astype(jnp.float32)
    partial = jnp.sum(values * values, axis=0, keepdims=True)
    squares = ring_sum(partial, "ch")
    letters = write_letters(
        long_filter.reshape(DEVICES, 2, 8, EIGHTHS * LANES), token_ids.reshape(EIGHTHS, LANES)
    )
    mail = lax.all_to_all(letters, "seq", split_axis=0, concat_axis=0, tiled=True)

    scale = 1.0 / jnp.sqrt(squares / MIXER_CHANNELS + EPSILON)
    own = lax.dynamic_slice_in_dim(projected, rank * CHANNELS, CHANNELS, axis=1)
    table = (own.astype(jnp.float32) * scale[None]).astype(jnp.bfloat16)

    own_taps = lax.dynamic_slice_in_dim(short_taps, rank * CHANNELS, CHANNELS, axis=2)
    taps = jnp.broadcast_to(own_taps.reshape(TAPS * 3, CHANNELS, 1), (TAPS * 3, CHANNELS, LANES))
    skip = lax.dynamic_slice_in_dim(skip_gain, rank * CHANNELS, CHANNELS)

    mixed = mix_tokens(skip, mail, table, taps)
    return lax.all_to_all(mixed, "seq", split_axis=0, concat_axis=0, tiled=True)


def solution(mesh):
    placed = (
        P("seq"),
        P("ch", None),
        P(None, "ch", None),
        P(None, None, "ch"),
        P("ch", "seq"),
        P("ch"),
    )
    return jax.shard_map(shards, mesh=mesh, in_specs=placed, out_specs=P("ch", "seq"), check_vma=False)
```
